128 devices in a mesh: group: 8 (over y_hi, z), tile: 16 (over x, y_lo, core).
Axes of the slice: x: 4, y: 4 (y_hi: 2, y_lo: 2; y = y_hi * 2 + y_lo), z: 4, core: 2. Of those that a mesh axis runs over, the one named last changes fastest.
Arguments:
- contrast: bfloat16 [8192, 1024], P('tile', 'group'), may hold values from -6 to 6
- incident: bfloat16 [8, 8, 8192, 1024], P('group', None, 'tile'), may hold values from -2.5 to 2.5
- signs: int32 [8, 8, 8], P('group'), may hold values from -1 to 1, as said below
- adjoint: bfloat16 [8, 8, 8192, 1024], P('group', None, 'tile'), may hold values from -1 to 1
- proj: bfloat16 [1024, 256], replicated, may hold values from -0.1875 to 0.1875
- mats: bfloat16 [6, 256, 256], replicated, may hold values from -0.15625 to 0.15625
- offsets: int32 [6], replicated, may hold values from -3 to 3, as said below
- expand: bfloat16 [256, 1024], replicated, may hold values from -0.375 to 0.375
Outputs:
- scattered: bfloat16 [8, 8, 8192, 1024], P('group', None, 'tile')
- gradient: float32 [8192, 1024], P('tile', 'group')
The draws below stay inside these ranges and needn't reach their ends.
Inputs may be any that keep to these rules, and one draw needn't show every extreme that they name: `signs`: each entry is -1 or 1. The offsets are distinct; -3 and 3 both occur.
All inputs are finite; a program needn't handle non-finite values.
Results may differ from the reference program's by a relative error of at most 0.015.
Values may be sent and summed in bfloat16 or wider, within the bound.
A program may use at most 192 MiB of HBM per device.

```python
import jax
import jax.numpy as jnp
from jax import lax

P_SIZE = 1024
K = 256
E = 8
S = 8
NOFF = 6
BOXES = 8192
GROUPS = 8


def draw_signs(key, part):
    return 2 * jax.random.randint(key, (GROUPS, E, S), 0, 2).astype(jnp.int32) - 1


def draw_offsets(key, part):
    inner = jax.random.permutation(key, jnp.arange(-2, 3, dtype=jnp.int32))
    ends = jnp.array([-3, 3], dtype=jnp.int32)
    return jnp.concatenate([ends, inner[:NOFF - 2]]).astype(jnp.int32)


def with_spikes(result, rng, source, target, parts, factor):
    def block_of(position):
        return (jnp.arange(result.shape[position]) // (result.shape[position] // parts)).reshape((-1,) + (1,) * (result.ndim - 1 - position))

    first = jax.random.permutation(rng, parts)[block_of(target)]
    far = (block_of(target) + parts // 2) % parts
    return jnp.where((block_of(source) == first) | (block_of(source) == far), factor * result, result)


def levels(rng, extent, split, least, largest):
    factor_of = 1.0
    for dim, parts in split:
        heights = jax.random.uniform(jax.random.fold_in(jax.random.fold_in(rng, 6), dim), (parts,), jnp.float32, least / len(split), largest / len(split))
        factor_of = factor_of * jnp.repeat(jnp.exp(heights), extent[dim] // parts).reshape((-1,) + (1,) * (len(extent) - 1 - dim))
    return factor_of


def centred(own_key, dims, deviation, bound, cuts=(), held_as=jnp.bfloat16):
    entries = jax.random.normal(own_key, dims, jnp.float32) * deviation
    if len(cuts) > 0:
        entries = levels(own_key, dims, cuts, -0.22, 0.18) * entries
    return jnp.clip(entries, min=-bound, max=bound).astype(held_as)


def heavy_noise(own_key, extent, width, bound, split, heavy, kind=jnp.bfloat16):
    values = width * jax.random.normal(own_key, extent, jnp.float32)
    if split:
        values = values * levels(own_key, extent, split, -0.22, 0.18)
    return jnp.clip(with_spikes(values, jax.random.fold_in(own_key, 3), *heavy), -bound, bound).astype(kind)


def setup_inputs(seed: int = 0) -> dict:
    streams_of = jax.random.split(jax.random.key(seed), 9)
    contrast = centred(streams_of[0], (BOXES, P_SIZE), 1.0, 6.0, ((0, 16), (1, 8)))
    incident = centred(streams_of[1], (GROUPS, S, BOXES, P_SIZE), 0.35, 2.5, ((0, 8), (2, 16)))
    signs = draw_signs(jax.random.fold_in(streams_of[8], 71), 0)
    adjoint = heavy_noise(streams_of[3], (GROUPS, E, BOXES, P_SIZE), 0.125, 1.0, ((0, 8), (2, 16)), (0, 3, 8, 2.0))
    proj = centred(streams_of[4], (P_SIZE, K), P_SIZE ** -0.5, 0.1875)
    mats = centred(streams_of[5], (NOFF, K, K), (K * NOFF) ** -0.5, 0.15625)
    offsets = draw_offsets(jax.random.fold_in(streams_of[8], 71), 0)
    expand = centred(streams_of[7], (K, P_SIZE), K ** -0.5, 0.375)
    return {"contrast": contrast, "incident": incident, "signs": signs, "adjoint": adjoint, "proj": proj, "mats": mats, "offsets": offsets, "expand": expand}


def reference(contrast, incident, signs, adjoint, proj, mats, offsets, expand):
    nbox = contrast.shape[0]
    cfl = contrast.astype(jnp.float32)

    def one_group(items):
        inc_g, sign_g, adj_g = items
        encoded = jnp.einsum("es,sbp->ebp", sign_g.astype(jnp.float32), inc_g.astype(jnp.float32)).astype(jnp.bfloat16)
        source = (cfl[None] * encoded.astype(jnp.float32)).astype(jnp.bfloat16)
        coeffs = jnp.dot(source.reshape(-1, P_SIZE), proj, preferred_element_type=jnp.float32).reshape(E, nbox, K).astype(jnp.bfloat16)
        padded = jnp.pad(coeffs, ((0, 0), (3, 3), (0, 0)))
        local = jnp.zeros((E, nbox, K), jnp.float32)
        for t in range(NOFF):
            start = (offsets[t] + 3).astype(jnp.int32)
            moved = lax.dynamic_slice_in_dim(padded, start, nbox, 1)
            local = local + jnp.dot(moved.reshape(-1, K), mats[t], preferred_element_type=jnp.float32).reshape(E, nbox, K)
        local = local.astype(jnp.bfloat16)
        field = jnp.dot(local.reshape(-1, K), expand, preferred_element_type=jnp.float32).reshape(E, nbox, P_SIZE)
        total = encoded.astype(jnp.float32) + field
        terms = jnp.sum(adj_g.astype(jnp.float32) * total, axis=0)
        return field.astype(jnp.bfloat16), terms

    scattered, terms = lax.map(one_group, (incident, signs, adjoint))
    return scattered, jnp.sum(terms, axis=0)
```

```python
import jax
import jax.numpy as jnp
from jax import lax
from jax.experimental import pallas as pl
from jax.experimental.pallas import tpu as pltpu
from jax.sharding import PartitionSpec as P

MESH = pl.DeviceIdType.MESH
BF = jnp.bfloat16
F32 = jnp.float32

S = 8
K = 256
PTS = 1024
NB = 512
HB = 32
TB = 64
NT = NB // TB
NG = 8
GW = PTS // NG
PAD = 8
CW = 256
NC = PTS // CW
REACH = 3
ND = 2 * REACH + 1


def scatter_gradient_kernel(
    signs, offsets, con_hbm, inc_hbm, adj_hbm, proj, mats, expand,
    loc_hbm, part_hbm,
    con_v, inc_v, enc_v, adj_v, coef_v, loc_v, term_v, kron, shifts,
    in_sem, con_sem, adj_sem, loc_sem, own_sem,
    ag_send, ag_recv, rs_send, rs_recv, halo_send, halo_recv,
):
    g = lax.axis_index("group")
    tile = lax.axis_index("tile")
    last = lax.axis_size("tile") - 1

    def rows_of(t):
        return pl.ds(pl.multiple_of(t * TB, TB), TB)

    def inc_copy(t):
        r = rows_of(t)
        return pltpu.make_async_copy(inc_hbm.at[:, r], inc_v.at[:, r], in_sem.at[t])

    def adj_copy(t):
        r = rows_of(t)
        return pltpu.make_async_copy(adj_hbm.at[:, r], adj_v.at[:, r], adj_sem.at[t])

    mine = pl.ds(pl.multiple_of(g * GW, GW), GW)
    con_copy = pltpu.make_async_copy(con_hbm, con_v.at[:, mine], con_sem)

    def ag_copy(t, k):
        return pltpu.make_async_remote_copy(
            src_ref=con_hbm.at[rows_of(t)],
            dst_ref=con_v.at[rows_of(t), mine],
            send_sem=ag_send.at[t, k - 1],
            recv_sem=ag_recv.at[t, k - 1],
            device_id=(lax.rem(g + k, NG), tile),
            device_id_type=MESH,
        )

    def rs_copy(t, k):
        peer = lax.rem(g + k, NG)
        return pltpu.make_async_remote_copy(
            src_ref=term_v.at[peer, rows_of(t)],
            dst_ref=part_hbm.at[g, rows_of(t)],
            send_sem=rs_send.at[t, k - 1],
            recv_sem=rs_recv.at[t, k - 1],
            device_id=(peer, tile),
            device_id_type=MESH,
        )

    def own_copy(t):
        r = rows_of(t)
        return pltpu.make_async_copy(term_v.at[g, r], part_hbm.at[g, r], own_sem.at[t])

    def loc_copy(t):
        r = rows_of(t)
        return pltpu.make_async_copy(loc_v.at[:, r], loc_hbm.at[:, r], loc_sem.at[t])

    def halo_up():
        return pltpu.make_async_remote_copy(
            src_ref=coef_v.at[:, pl.ds(NB, PAD)],
            dst_ref=coef_v.at[:, pl.ds(0, PAD)],
            send_sem=halo_send.at[0],
            recv_sem=halo_recv.at[0],
            device_id=(g, tile + 1),
            device_id_type=MESH,
        )

    def halo_down():
        return pltpu.make_async_remote_copy(
            src_ref=coef_v.at[:, pl.ds(PAD, PAD)],
            dst_ref=coef_v.at[:, pl.ds(NB + PAD, PAD)],
            send_sem=halo_send.at[1],
            recv_sem=halo_recv.at[1],
            device_id=(g, tile - 1),
            device_id_type=MESH,
        )

    def tile_at(j):
        return jnp.where(j == 0, 0, jnp.where(j == 1, NT - 1, j - 1))

    con_copy.start()
    inc_copy(0).start()
    inc_copy(NT - 1).start()
    for t in range(1, NT - 1):
        inc_copy(t).start()
    for t in list(range(1, NT - 1)) + [0, NT - 1]:
        adj_copy(t).start()

    barrier = pltpu.get_barrier_semaphore()
    for k in range(1, NG):
        pl.semaphore_signal(
            barrier, inc=1, device_id=(lax.rem(g + k, NG), tile), device_id_type=MESH
        )

    for step_of in (1, last):
        pl.semaphore_signal(
            barrier, inc=1, device_id=(g, lax.rem(tile + step_of, last + 1)), device_id_type=MESH
        )
    pl.semaphore_wait(barrier, NG + 1)

    def ag_start(j, carry):
        for k in range(1, NG):
            ag_copy(tile_at(j), k).start()
        return carry

    lax.fori_loop(0, NT, ag_start, 0)

    lane = lax.broadcasted_iota(jnp.int32, (HB, S * HB), 1)
    row = lax.broadcasted_iota(jnp.int32, (HB, S * HB), 0)
    diag = lax.rem(lane, HB) == row
    source = lane // HB
    for e in range(S):
        value = jnp.zeros((HB, S * HB), F32)
        for s in range(S):
            value = jnp.where(source == s, signs[e, s].astype(F32), value)
        kron[pl.ds(e * HB, HB), :] = jnp.where(diag, value, 0.0).astype(BF)

    for d in range(ND):
        found = jnp.int32(0)
        where = jnp.int32(0)
        for t in range(mats.shape[0]):
            hit = offsets[t] == d - REACH
            found = jnp.where(hit, 1, found)
            where = jnp.where(hit, t, where)
        shifts[d] = (mats[where].astype(F32) * found.astype(F32)).astype(BF)

    @pl.when(tile == 0)
    def _():
        coef_v[:, 0:PAD, :] = jnp.zeros((S, PAD, K), F32)

    @pl.when(tile == last)
    def _():
        coef_v[:, NB + PAD : NB + 2 * PAD, :] = jnp.zeros((S, PAD, K), F32)

    con_copy.wait()

    def project(t):
        inc_copy(t).wait()
        for k in range(1, NG):
            ag_copy(t, k).wait_recv()
        for h in range(TB // HB):
            b0 = pl.multiple_of(t * TB + h * HB, HB)
            boxes = pl.ds(b0, HB)
            acc = jnp.zeros((S * HB, K), F32)
            for c in range(NC):
                cols = pl.ds(c * CW, CW)
                enc = jnp.dot(
                    kron[...],
                    inc_v[:, boxes, cols].reshape(S * HB, CW),
                    preferred_element_type=F32,
                ).astype(BF).reshape(S, HB, CW)
                enc_v[:, boxes, cols] = enc
                src = enc * con_v[boxes, cols][None]
                acc = acc + jnp.dot(
                    src.reshape(S * HB, CW), proj[cols, :], preferred_element_type=F32
                )
            coef_v[:, pl.ds(pl.multiple_of(b0 + PAD, PAD), HB), :] = acc.reshape(S, HB, K)

    def expand_terms(t):
        adj_copy(t).wait()
        for h in range(TB // HB):
            b0 = pl.multiple_of(t * TB + h * HB, HB)
            boxes = pl.ds(b0, HB)
            acc = jnp.zeros((S * HB, K), F32)
            window = coef_v.at[:, pl.ds(b0, HB + 2 * PAD), :]
            for d in range(ND):
                first = PAD + d - REACH
                moved = window[:, first : first + HB, :]
                acc = acc + jnp.dot(
                    moved.astype(BF).reshape(S * HB, K), shifts[d], preferred_element_type=F32
                )
            local = acc.astype(BF)
            loc_v[:, boxes, :] = local.reshape(S, HB, K)
            for c in range(NC):
                cols = pl.ds(c * CW, CW)
                field = jnp.dot(local, expand[:, cols], preferred_element_type=F32)
                total = enc_v[:, boxes, cols].astype(F32) + field.reshape(S, HB, CW)
                term = jnp.sum(adj_v[:, boxes, cols].astype(F32) * total, axis=0).astype(BF)
                for q in range(CW // GW):
                    term_v[c * (CW // GW) + q, boxes, :] = term[:, q * GW : (q + 1) * GW]
        loc_copy(t).start()
        own_copy(t).start()
        for k in range(1, NG):
            rs_copy(t, k).start()

    def step(j, carry):
        @pl.when(j < NT)
        def _():
            project(tile_at(j))

        @pl.when(j == 2)
        def _():
            @pl.when(tile < last)
            def _():
                halo_up().start()

            @pl.when(tile > 0)
            def _():
                halo_down().start()

        @pl.when(j == NT + 1)
        def _():
            @pl.when(tile > 0)
            def _():
                halo_up().wait_recv()

            @pl.when(tile < last)
            def _():
                halo_down().wait_recv()

        @pl.when(j >= 3)
        def _():
            expand_terms(jnp.where(j == NT + 1, 0, jnp.where(j == NT + 2, NT - 1, j - 2)))

        return carry

    lax.fori_loop(0, NT + 3, step, 0)

    def finish(t, carry):
        loc_copy(t).wait()
        own_copy(t).wait()
        for k in range(1, NG):
            ag_copy(t, k).wait_send()
            rs_copy(t, k).wait_send()
            rs_copy(t, k).wait_recv()
        return carry

    lax.fori_loop(0, NT, finish, 0)

    @pl.when(tile < last)
    def _():
        halo_up().wait_send()

    @pl.when(tile > 0)
    def _():
        halo_down().wait_send()


def output_kernel(loc, expand, part, scat, grad):
    n = loc.shape[1]
    for c in range(NC):
        cols = pl.ds(c * CW, CW)
        scat[:, :, cols] = (
            jnp.dot(loc[...].reshape(S * n, K), expand[:, cols], preferred_element_type=F32)
            .astype(BF)
            .reshape(S, n, CW)
        )
    grad[...] = jnp.sum(part[...].astype(F32), axis=0)


def on_device(contrast, incident, signs, adjoint, proj, mats, offsets, expand):
    any_spec = pl.BlockSpec(memory_space=pl.ANY)
    vmem = pl.BlockSpec(memory_space=pltpu.VMEM)
    smem = pl.BlockSpec(memory_space=pltpu.SMEM)
    dma = pltpu.SemaphoreType.DMA
    local, parts = pl.pallas_call(
        scatter_gradient_kernel,
        out_shape=(
            jax.ShapeDtypeStruct((S, NB, K), BF),
            jax.ShapeDtypeStruct((NG, NB, GW), BF),
        ),
        in_specs=[smem, smem, any_spec, any_spec, any_spec, vmem, vmem, vmem],
        out_specs=(any_spec, any_spec),
        scratch_shapes=[
            pltpu.VMEM((NB, PTS), BF),
            pltpu.VMEM((S, NB, PTS), BF),
            pltpu.VMEM((S, NB, PTS), BF),
            pltpu.VMEM((S, NB, PTS), BF),
            pltpu.VMEM((S, NB + 2 * PAD, K), F32),
            pltpu.VMEM((S, NB, K), BF),
            pltpu.VMEM((NG, NB, GW), BF),
            pltpu.VMEM((S * HB, S * HB), BF),
            pltpu.VMEM((ND, K, K), BF),
            dma((NT,)),
            dma,
            dma((NT,)),
            dma((NT,)),
            dma((NT,)),
            dma((NT, NG - 1)),
            dma((NT, NG - 1)),
            dma((NT, NG - 1)),
            dma((NT, NG - 1)),
            dma((2,)),
            dma((2,)),
        ],
        compiler_params=pltpu.CompilerParams(
            collective_id=0, has_side_effects=True, vmem_limit_bytes=60 << 20
        ),
    )(signs[0], offsets, contrast, incident[0], adjoint[0], proj, mats, expand)

    scattered, gradient = pl.pallas_call(
        output_kernel,
        grid=(NT,),
        out_shape=(
            jax.ShapeDtypeStruct((S, NB, PTS), BF),
            jax.ShapeDtypeStruct((NB, GW), F32),
        ),
        in_specs=[
            pl.BlockSpec((S, TB, K), lambda i: (0, i, 0)),
            pl.BlockSpec((K, PTS), lambda i: (0, 0)),
            pl.BlockSpec((NG, TB, GW), lambda i: (0, i, 0)),
        ],
        out_specs=(
            pl.BlockSpec((S, TB, PTS), lambda i: (0, i, 0)),
            pl.BlockSpec((TB, GW), lambda i: (i, 0)),
        ),
        compiler_params=pltpu.CompilerParams(vmem_limit_bytes=60 << 20),
    )(local, expand, parts)
    return scattered[None], gradient


def solution(mesh):
    in_specs = (
        P("tile", "group"),
        P("group", None, "tile", None),
        P("group", None, None),
        P("group", None, "tile", None),
        P(),
        P(),
        P(),
        P(),
    )
    out_specs = (P("group", None, "tile", None), P("tile", "group"))
    return jax.shard_map(
        on_device, mesh=mesh, in_specs=in_specs, out_specs=out_specs, check_vma=False
    )
```

```python
import jax
import jax.numpy as jnp
from jax import lax
from jax.experimental import pallas as pl
from jax.experimental.pallas import tpu as pltpu
from jax.sharding import PartitionSpec as P

MESH = pl.DeviceIdType.MESH
BF = jnp.bfloat16
F32 = jnp.float32

S = 8
K = 256
PTS = 1024
NB = 512
HB = 32
ROWS = S * HB
TB = 64
NT = NB // TB
NG = 8
GW = PTS // NG
CW = 256
NC = PTS // CW
REACH = 3


def mm(a, b):
    return jnp.dot(a, b, preferred_element_type=F32)


def scatter_gradient_kernel(
    signs, offsets, con_hbm, inc_hbm, adj_hbm, proj, mats, expand,
    loc_hbm, part_hbm,
    con_v, inc_v, adj_v, coef_v, low_v, high_v, loc_v, first_v, term_v, enc_points, enc_coeffs, perm,
    in_sem, con_sem, adj_sem, loc_sem, own_sem,
    ag_send, ag_recv, rs_send, rs_recv, halo_send, halo_recv,
):
    g = lax.axis_index("group")
    tile = lax.axis_index("tile")
    last = lax.axis_size("tile") - 1

    def rows_of(t):
        return pl.ds(pl.multiple_of(t * TB, TB), TB)

    def inc_copy(t):
        r = rows_of(t)
        return pltpu.make_async_copy(inc_hbm.at[:, r], inc_v.at[:, r], in_sem.at[t])

    def adj_copy(t):
        r = rows_of(t)
        return pltpu.make_async_copy(adj_hbm.at[:, r], adj_v.at[:, r], adj_sem.at[t])

    mine = pl.ds(pl.multiple_of(g * GW, GW), GW)
    con_copy = pltpu.make_async_copy(con_hbm, con_v.at[:, mine], con_sem)

    def ag_copy(t, k):
        return pltpu.make_async_remote_copy(
            src_ref=con_hbm.at[rows_of(t)],
            dst_ref=con_v.at[rows_of(t), mine],
            send_sem=ag_send.at[t, k - 1],
            recv_sem=ag_recv.at[t, k - 1],
            device_id=(lax.rem(g + k, NG), tile),
            device_id_type=MESH,
        )

    def rs_copy(t, k):
        peer = lax.rem(g + k, NG)
        return pltpu.make_async_remote_copy(
            src_ref=term_v.at[peer, rows_of(t)],
            dst_ref=part_hbm.at[g, rows_of(t)],
            send_sem=rs_send.at[t, k - 1],
            recv_sem=rs_recv.at[t, k - 1],
            device_id=(peer, tile),
            device_id_type=MESH,
        )

    def own_copy(t):
        r = rows_of(t)
        return pltpu.make_async_copy(term_v.at[g, r], part_hbm.at[g, r], own_sem.at[t])

    def loc_copy(t):
        r = rows_of(t)
        return pltpu.make_async_copy(loc_v.at[:, r], loc_hbm.at[:, r], loc_sem.at[t])

    def halo_up():
        return pltpu.make_async_remote_copy(
            src_ref=coef_v.at[pl.ds(NB, REACH)],
            dst_ref=low_v,
            send_sem=halo_send.at[0],
            recv_sem=halo_recv.at[0],
            device_id=(g, tile + 1),
            device_id_type=MESH,
        )

    def halo_down():
        return pltpu.make_async_remote_copy(
            src_ref=coef_v.at[pl.ds(REACH, REACH)],
            dst_ref=high_v,
            send_sem=halo_send.at[1],
            recv_sem=halo_recv.at[1],
            device_id=(g, tile - 1),
            device_id_type=MESH,
        )

    def tile_at(j):
        return jnp.where(j == 0, 0, jnp.where(j == 1, NT - 1, j - 1))

    con_copy.start()
    for t in [0, NT - 1] + list(range(1, NT - 1)):
        inc_copy(t).start()
        adj_copy(t).start()

    barrier = pltpu.get_barrier_semaphore()
    for k in range(1, NG):
        pl.semaphore_signal(
            barrier, inc=1, device_id=(lax.rem(g + k, NG), tile), device_id_type=MESH
        )
    for step_of in (1, last):
        pl.semaphore_signal(
            barrier, inc=1, device_id=(g, lax.rem(tile + step_of, last + 1)), device_id_type=MESH
        )

    lane8 = lax.broadcasted_iota(jnp.int32, (S, ROWS), 1)
    row8 = lax.broadcasted_iota(jnp.int32, (S, ROWS), 0)
    sign = jnp.zeros((S, ROWS), F32)
    for e in range(S):
        for s in range(S):
            here = (row8 == e) & (lane8 // HB == s)
            sign = jnp.where(here, signs[e, s].astype(F32), sign)
    for b in range(0, HB, 2):
        pair = [jnp.where(lax.rem(lane8, HB) == b + i, sign, 0.0) for i in range(2)]
        enc_coeffs[pl.ds(b * S, 2 * S), :] = jnp.concatenate(pair, axis=0).astype(BF)
    lane = lax.broadcasted_iota(jnp.int32, (HB, ROWS), 1)
    row = lax.broadcasted_iota(jnp.int32, (HB, ROWS), 0)
    for e in range(S):
        wide = jnp.broadcast_to(sign[e : e + 1, :], (HB, ROWS))
        enc_points[pl.ds(e * HB, HB), :] = jnp.where(lax.rem(lane, HB) == row, wide, 0.0).astype(BF)
        there = (lane // S == row) & (lax.rem(lane, S) == e)
        perm[pl.ds(e * HB, HB), :] = jnp.where(there, 1.0, 0.0).astype(BF)

    pl.semaphore_wait(barrier, NG + 1)

    def ag_start(j, carry):
        for k in range(1, NG):
            ag_copy(tile_at(j), k).start()
        return carry

    lax.fori_loop(0, NT, ag_start, 0)

    def halves(t):
        for h in range(TB // HB):
            b0 = pl.multiple_of(t * TB + h * HB, HB)
            yield b0, pl.ds(b0, HB)

    def weighted(boxes, cols, field):
        adj = adj_v[:, boxes, cols].astype(F32)
        return jnp.sum(adj * field.reshape(S, HB, CW), axis=0)

    def encode(j, carry):
        t = tile_at(j)
        inc_copy(t).wait()
        adj_copy(t).wait()
        for b0, boxes in halves(t):
            for c in range(NC):
                cols = pl.ds(c * CW, CW)
                enc = mm(enc_points[...], inc_v[:, boxes, cols].reshape(ROWS, CW))
                first_v[boxes, cols] = weighted(boxes, cols, enc)
        return carry

    lax.fori_loop(0, NT, encode, 0)
    con_copy.wait()

    def project(t):
        for k in range(1, NG):
            ag_copy(t, k).wait_recv()
        sums = []
        for b0, boxes in halves(t):
            acc = jnp.zeros((ROWS, K), F32)
            for c in range(NC):
                cols = pl.ds(c * CW, CW)
                src = inc_v[:, boxes, cols] * con_v[boxes, cols][None]
                acc = acc + mm(src.reshape(ROWS, CW), proj[cols, :])
            sums.append(acc.astype(BF))
        for (b0, boxes), acc in zip(halves(t), sums):
            coef = mm(enc_coeffs[...], acc).astype(BF)
            coef_v[pl.ds(b0 + REACH, HB)] = coef.reshape(HB, S, K)

    def expand_terms(t):
        sums = []
        for b0, boxes in halves(t):
            acc = jnp.zeros((ROWS, K), F32)
            for i in range(mats.shape[0]):
                moved = coef_v[pl.ds(b0 + REACH + offsets[i], HB)]
                acc = acc + mm(moved.reshape(ROWS, K), mats[i])
            sums.append(acc.astype(BF))
        locals_ = [mm(perm[...], acc).astype(BF) for acc in sums]
        for (b0, boxes), local in zip(halves(t), locals_):
            loc_v[:, boxes, :] = local.reshape(S, HB, K)
            for c in range(NC):
                cols = pl.ds(c * CW, CW)
                field = mm(local, expand[:, cols])
                term = (weighted(boxes, cols, field) + first_v[boxes, cols]).astype(BF)
                for q in range(CW // GW):
                    term_v[c * (CW // GW) + q, boxes, :] = term[:, q * GW : (q + 1) * GW]
        loc_copy(t).start()
        own_copy(t).start()
        for k in range(1, NG):
            rs_copy(t, k).start()

    def step(j, carry):
        @pl.when(j < NT)
        def _():
            project(tile_at(j))

        @pl.when(j == 2)
        def _():
            @pl.when(tile < last)
            def _():
                halo_up().start()

            @pl.when(tile > 0)
            def _():
                halo_down().start()

        @pl.when(j == NT + 1)
        def _():
            @pl.when(tile > 0)
            def _():
                halo_up().wait_recv()
                coef_v[pl.ds(0, REACH)] = low_v[...]

            @pl.when(tile == 0)
            def _():
                coef_v[pl.ds(0, REACH)] = jnp.zeros((REACH, S, K), BF)

            @pl.when(tile < last)
            def _():
                halo_down().wait_recv()
                coef_v[pl.ds(NB + REACH, REACH)] = high_v[...]

            @pl.when(tile == last)
            def _():
                coef_v[pl.ds(NB + REACH, REACH)] = jnp.zeros((REACH, S, K), BF)

        @pl.when(j >= 3)
        def _():
            expand_terms(jnp.where(j == NT + 1, 0, jnp.where(j == NT + 2, NT - 1, j - 2)))

        return carry

    lax.fori_loop(0, NT + 3, step, 0)

    def finish(t, carry):
        loc_copy(t).wait()
        own_copy(t).wait()
        for k in range(1, NG):
            ag_copy(t, k).wait_send()
            rs_copy(t, k).wait_send()
            rs_copy(t, k).wait_recv()
        return carry

    lax.fori_loop(0, NT, finish, 0)

    @pl.when(tile < last)
    def _():
        halo_up().wait_send()

    @pl.when(tile > 0)
    def _():
        halo_down().wait_send()


def output_kernel(loc, expand, part, scat, grad):
    n = loc.shape[1]
    for c in range(NC):
        cols = pl.ds(c * CW, CW)
        scat[:, :, cols] = (
            mm(loc[...].reshape(S * n, K), expand[:, cols]).astype(BF).reshape(S, n, CW)
        )
    grad[...] = jnp.sum(part[...].astype(F32), axis=0)


def on_device(contrast, incident, signs, adjoint, proj, mats, offsets, expand):
    any_spec = pl.BlockSpec(memory_space=pl.ANY)
    vmem = pl.BlockSpec(memory_space=pltpu.VMEM)
    smem = pl.BlockSpec(memory_space=pltpu.SMEM)
    dma = pltpu.SemaphoreType.DMA
    local, parts = pl.pallas_call(
        scatter_gradient_kernel,
        out_shape=(
            jax.ShapeDtypeStruct((S, NB, K), BF),
            jax.ShapeDtypeStruct((NG, NB, GW), BF),
        ),
        in_specs=[smem, smem, any_spec, any_spec, any_spec, vmem, vmem, vmem],
        out_specs=(any_spec, any_spec),
        scratch_shapes=[
            pltpu.VMEM((NB, PTS), BF),
            pltpu.VMEM((S, NB, PTS), BF),
            pltpu.VMEM((S, NB, PTS), BF),
            pltpu.VMEM((NB + 2 * REACH, S, K), BF),
            pltpu.VMEM((REACH, S, K), BF),
            pltpu.VMEM((REACH, S, K), BF),
            pltpu.VMEM((S, NB, K), BF),
            pltpu.VMEM((NB, PTS), F32),
            pltpu.VMEM((NG, NB, GW), BF),
            pltpu.VMEM((ROWS, ROWS), BF),
            pltpu.VMEM((ROWS, ROWS), BF),
            pltpu.VMEM((ROWS, ROWS), BF),
            dma((NT,)),
            dma,
            dma((NT,)),
            dma((NT,)),
            dma((NT,)),
            dma((NT, NG - 1)),
            dma((NT, NG - 1)),
            dma((NT, NG - 1)),
            dma((NT, NG - 1)),
            dma((2,)),
            dma((2,)),
        ],
        compiler_params=pltpu.CompilerParams(
            collective_id=0, has_side_effects=True, vmem_limit_bytes=60 << 20
        ),
    )(signs[0], offsets, contrast, incident[0], adjoint[0], proj, mats, expand)

    scattered, gradient = pl.pallas_call(
        output_kernel,
        grid=(NT,),
        out_shape=(
            jax.ShapeDtypeStruct((S, NB, PTS), BF),
            jax.ShapeDtypeStruct((NB, GW), F32),
        ),
        in_specs=[
            pl.BlockSpec((S, TB, K), lambda i: (0, i, 0)),
            pl.BlockSpec((K, PTS), lambda i: (0, 0)),
            pl.BlockSpec((NG, TB, GW), lambda i: (0, i, 0)),
        ],
        out_specs=(
            pl.BlockSpec((S, TB, PTS), lambda i: (0, i, 0)),
            pl.BlockSpec((TB, GW), lambda i: (i, 0)),
        ),
        compiler_params=pltpu.CompilerParams(vmem_limit_bytes=60 << 20),
    )(local, expand, parts)
    return scattered[None], gradient


def solution(mesh):
    in_specs = (
        P("tile", "group"),
        P("group", None, "tile", None),
        P("group", None, None),
        P("group", None, "tile", None),
        P(),
        P(),
        P(),
        P(),
    )
    out_specs = (P("group", None, "tile", None), P("tile", "group"))
    return jax.shard_map(
        on_device, mesh=mesh, in_specs=in_specs, out_specs=out_specs, check_vma=False
    )
```

```python
import jax
import jax.numpy as jnp
from jax import lax
from jax.experimental import pallas as pl
from jax.experimental.pallas import tpu as pltpu
from jax.sharding import PartitionSpec as P

MESH = pl.DeviceIdType.MESH
BF = jnp.bfloat16
F32 = jnp.float32

S = 8
K = 256
PTS = 1024
NB = 512
HB = 32
ROWS = S * HB
TB = 64
NT = NB // TB
NG = 8
GW = PTS // NG
CW = 256
NC = PTS // CW
REACH = 3
NZ = 4
CB = 128
NCH = NB // CB


def mm(a, b):
    return jnp.dot(a, b, preferred_element_type=F32)


def scatter_gradient_kernel(
    signs, offsets, con_hbm, inc_hbm, adj_hbm, proj, mats, expand,
    loc_hbm, part_hbm,
    con_v, inc_v, adj_v, coef_v, low_v, high_v, loc_v, first_v, term_v, stage_v, sum_v, own_v,
    enc_points, enc_coeffs, perm,
    in_sem, adj_sem, one_sem,
    ag_send, ag_recv, rs_send, rs_recv, halo_send, halo_recv,
):
    g = lax.axis_index("group")
    tile = lax.axis_index("tile")
    last = lax.axis_size("tile") - 1
    half = g // NZ
    z = lax.rem(g, NZ)
    partner = lax.rem(g + NZ, NG)

    def z_at(dz):
        return lax.rem(z + dz, NZ)

    def z_peer(dz):
        return half * NZ + z_at(dz)

    def rows_of(t):
        return pl.ds(pl.multiple_of(t * TB, TB), TB)

    def chunk_of(c):
        return pl.ds(pl.multiple_of(c * CB, CB), CB)

    def inc_copy(t):
        r = rows_of(t)
        return pltpu.make_async_copy(inc_hbm.at[:, r], inc_v.at[:, r], in_sem.at[t])

    def adj_copy(t):
        r = rows_of(t)
        return pltpu.make_async_copy(adj_hbm.at[:, r], adj_v.at[:, r], adj_sem.at[t])

    def remote(src, dst, send, recv, group, at=tile):
        return pltpu.make_async_remote_copy(
            src_ref=src,
            dst_ref=dst,
            send_sem=send,
            recv_sem=recv,
            device_id=(group, at),
            device_id_type=MESH,
        )

    con_copy = pltpu.make_async_copy(con_hbm, con_v.at[g], one_sem.at[0])
    own_copy = pltpu.make_async_copy(own_v, part_hbm.at[0], one_sem.at[1])
    loc_most = pl.ds(TB, NB - TB)
    loc_copies = [
        pltpu.make_async_copy(loc_v.at[:, r], loc_hbm.at[:, r], one_sem.at[2 + i])
        for i, r in enumerate((loc_most, pl.ds(0, TB)))
    ]

    def ag_direct(c, q):
        r = chunk_of(c)
        to = partner if q == 0 else z_peer(q)
        return remote(con_hbm.at[r], con_v.at[g, r], ag_send.at[c, q], ag_recv.at[c, q], to)

    def ag_relay(c, dz, even):
        r = chunk_of(c)
        held = con_v.at[partner if even else z_peer(NZ - dz), r]
        to = z_peer(dz) if even else partner
        return remote(held, held, ag_send.at[c, NZ - 1 + dz], ag_recv.at[c, NZ - 1 + dz], to)

    def gather_start(c):
        for q in range(NZ):
            ag_direct(c, q).start()

    def gather_pass(c, even):
        if even:
            ag_direct(c, 0).wait_recv()
        for dz in range(1, NZ):
            if not even:
                ag_direct(c, dz).wait_recv()
            ag_relay(c, dz, even).start()

    def gather_wait(c, even):
        for q in range(1, NZ) if even else (0,):
            ag_direct(c, q).wait_recv()
        for dz in range(1, NZ):
            ag_relay(c, dz, even).wait_recv()

    def z_terms(t, dz):
        r = rows_of(t)
        dst = stage_v.at[pl.ds(2 * (dz - 1), 2), r]
        return remote(term_v.at[z_at(dz), :, r], dst, rs_send.at[t, dz], rs_recv.at[t, dz], z_peer(dz))

    def z_sums(t):
        r = rows_of(t)
        return remote(sum_v.at[0, r], part_hbm.at[1, r], rs_send.at[t, 0], rs_recv.at[t, 0], partner)

    def half_terms(t):
        r = rows_of(t)
        dst = stage_v.at[pl.ds(0, NZ), r]
        return remote(term_v.at[:, 1 - half, r], dst, rs_send.at[t, 0], rs_recv.at[t, 0], partner)

    def half_sums(t, dz):
        r = rows_of(t)
        return remote(
            sum_v.at[z_at(dz), r], part_hbm.at[dz, r], rs_send.at[t, dz], rs_recv.at[t, dz], z_peer(dz)
        )

    def terms_start(t):
        even = lax.rem(t, 2) == 0

        @pl.when(even)
        def _():
            for dz in range(1, NZ):
                z_terms(t, dz).start()

        @pl.when(jnp.logical_not(even))
        def _():
            half_terms(t).start()

    def terms_pass(t):
        even = lax.rem(t, 2) == 0
        r = rows_of(t)

        @pl.when(even)
        def _():
            for dz in range(1, NZ):
                z_terms(t, dz).wait_recv()
            for h, out in ((half, own_v), (1 - half, sum_v.at[0])):
                total = term_v[z, h, r].astype(F32)
                for i in range(NZ - 1):
                    total = total + stage_v[2 * i + h, r].astype(F32)
                out[r] = total.astype(BF)
            z_sums(t).start()

        @pl.when(jnp.logical_not(even))
        def _():
            half_terms(t).wait_recv()
            for dz in range(NZ):
                to = z_at(dz)
                total = (term_v[to, half, r].astype(F32) + stage_v[to, r].astype(F32)).astype(BF)
                if dz == 0:
                    own_v[r] = total
                else:
                    sum_v[to, r] = total
            for dz in range(1, NZ):
                half_sums(t, dz).start()

    def halo_up():
        return remote(coef_v.at[pl.ds(NB, REACH)], low_v, halo_send.at[0], halo_recv.at[0], g, tile + 1)

    def halo_down():
        return remote(coef_v.at[pl.ds(REACH, REACH)], high_v, halo_send.at[1], halo_recv.at[1], g, tile - 1)

    for t in range(NT):
        inc_copy(t).start()
        adj_copy(t).start()
    con_copy.start()

    barrier = pltpu.get_barrier_semaphore()
    for to in [partner] + [z_peer(dz) for dz in range(1, NZ)]:
        pl.semaphore_signal(barrier, inc=1, device_id=(to, tile), device_id_type=MESH)
    for step_of in (1, last):
        pl.semaphore_signal(
            barrier, inc=1, device_id=(g, lax.rem(tile + step_of, last + 1)), device_id_type=MESH
        )

    lane8 = lax.broadcasted_iota(jnp.int32, (S, ROWS), 1)
    row8 = lax.broadcasted_iota(jnp.int32, (S, ROWS), 0)
    sign = jnp.zeros((S, ROWS), F32)
    for e in range(S):
        for s in range(S):
            here = (row8 == e) & (lane8 // HB == s)
            sign = jnp.where(here, signs[e, s].astype(F32), sign)
    for b in range(0, HB, 2):
        pair = [jnp.where(lax.rem(lane8, HB) == b + i, sign, 0.0) for i in range(2)]
        enc_coeffs[pl.ds(b * S, 2 * S), :] = jnp.concatenate(pair, axis=0).astype(BF)
    lane = lax.broadcasted_iota(jnp.int32, (HB, ROWS), 1)
    row = lax.broadcasted_iota(jnp.int32, (HB, ROWS), 0)
    for e in range(S):
        wide = jnp.broadcast_to(sign[e : e + 1, :], (HB, ROWS))
        enc_points[pl.ds(e * HB, HB), :] = jnp.where(lax.rem(lane, HB) == row, wide, 0.0).astype(BF)
        there = (lane // S == row) & (lax.rem(lane, S) == e)
        perm[pl.ds(e * HB, HB), :] = jnp.where(there, 1.0, 0.0).astype(BF)

    pl.semaphore_wait(barrier, NZ + 2)
    gather_start(0)
    gather_start(1)

    def halves(t):
        for h in range(TB // HB):
            b0 = pl.multiple_of(t * TB + h * HB, HB)
            yield b0, pl.ds(b0, HB)

    def weighted(boxes, cols, field):
        adj = adj_v[:, boxes, cols].astype(F32)
        return jnp.sum(adj * field.reshape(S, HB, CW), axis=0)

    def encode(t, carry):
        inc_copy(t).wait()
        adj_copy(t).wait()
        for b0, boxes in halves(t):
            for c in range(NC):
                cols = pl.ds(c * CW, CW)
                enc = mm(enc_points[...], inc_v[:, boxes, cols].reshape(ROWS, CW))
                first_v[boxes, cols] = weighted(boxes, cols, enc)

        @pl.when(t == NT - 2)
        def _():
            gather_pass(0, True)
            gather_start(2)

        return carry

    lax.fori_loop(0, NT, encode, 0)
    con_copy.wait()
    gather_pass(1, False)
    gather_start(3)

    def project(t):
        sums = []
        for b0, boxes in halves(t):
            acc = jnp.zeros((ROWS, K), F32)
            for c in range(NC):
                cols = pl.ds(c * CW, CW)
                pieces = [con_v[c * (CW // GW) + q, boxes] for q in range(CW // GW)]
                src = inc_v[:, boxes, cols] * jnp.concatenate(pieces, axis=1)[None]
                acc = acc + mm(src.reshape(ROWS, CW), proj[cols, :])
            sums.append(acc.astype(BF))
        for (b0, boxes), acc in zip(halves(t), sums):
            coef = mm(enc_coeffs[...], acc).astype(BF)
            coef_v[pl.ds(b0 + REACH, HB)] = coef.reshape(HB, S, K)

    def expand_terms(t):
        sums = []
        for b0, boxes in halves(t):
            acc = jnp.zeros((ROWS, K), F32)
            for i in range(mats.shape[0]):
                moved = coef_v[pl.ds(b0 + REACH + offsets[i], HB)]
                acc = acc + mm(moved.reshape(ROWS, K), mats[i])
            sums.append(acc.astype(BF))
        locals_ = [mm(perm[...], acc).astype(BF) for acc in sums]
        for (b0, boxes), local in zip(halves(t), locals_):
            loc_v[:, boxes, :] = local.reshape(S, HB, K)
            for c in range(NC):
                cols = pl.ds(c * CW, CW)
                field = mm(local, expand[:, cols])
                term = (weighted(boxes, cols, field) + first_v[boxes, cols]).astype(BF)
                for q in range(CW // GW):
                    h, to = divmod(c * (CW // GW) + q, NZ)
                    term_v[to, h, boxes, :] = term[:, q * GW : (q + 1) * GW]

    def step(j, carry):
        for c in range(NCH):

            @pl.when(j == c * (CB // TB))
            def _():
                gather_wait(c, c % 2 == 0)

        @pl.when(j < NT)
        def _():
            project(j)

        for c in range(2, NCH):

            @pl.when(j == c - 1)
            def _():
                gather_pass(c, c % 2 == 0)

        @pl.when(j == 1)
        def _():
            @pl.when(tile > 0)
            def _():
                halo_down().start()

        @pl.when(j == NT - 1)
        def _():
            @pl.when(tile < last)
            def _():
                halo_up().start()

        @pl.when(j == NT)
        def _():
            @pl.when(tile < last)
            def _():
                halo_down().wait_recv()
                coef_v[pl.ds(NB + REACH, REACH)] = high_v[...]

            @pl.when(tile == last)
            def _():
                coef_v[pl.ds(NB + REACH, REACH)] = jnp.zeros((REACH, S, K), BF)

        @pl.when(j == NT + 1)
        def _():
            loc_copies[0].start()

            @pl.when(tile > 0)
            def _():
                halo_up().wait_recv()
                coef_v[pl.ds(0, REACH)] = low_v[...]

            @pl.when(tile == 0)
            def _():
                coef_v[pl.ds(0, REACH)] = jnp.zeros((REACH, S, K), BF)

        @pl.when((j >= 2) & (j <= NT + 1))
        def _():
            t = jnp.where(j == NT + 1, 0, j - 1)
            expand_terms(t)
            terms_start(t)

        @pl.when(j == NT + 1)
        def _():
            loc_copies[1].start()

        @pl.when(j >= 4)
        def _():
            terms_pass(jnp.where(j == NT + 3, 0, j - 3))

        return carry

    lax.fori_loop(0, NT + 4, step, 0)
    own_copy.start()

    for c in range(NCH):
        for q in range(NZ):
            ag_direct(c, q).wait_send()
        for dz in range(1, NZ):
            ag_relay(c, dz, c % 2 == 0).wait_send()

    def finish(t, carry):
        even = lax.rem(t, 2) == 0

        @pl.when(even)
        def _():
            for dz in range(1, NZ):
                z_terms(t, dz).wait_send()
            z_sums(t).wait()

        @pl.when(jnp.logical_not(even))
        def _():
            half_terms(t).wait_send()
            for dz in range(1, NZ):
                half_sums(t, dz).wait()

        return carry

    lax.fori_loop(0, NT, finish, 0)
    for copy in loc_copies:
        copy.wait()
    own_copy.wait()

    @pl.when(tile < last)
    def _():
        halo_up().wait_send()

    @pl.when(tile > 0)
    def _():
        halo_down().wait_send()


def output_kernel(loc, expand, part, scat, grad):
    n = loc.shape[1]
    for c in range(NC):
        cols = pl.ds(c * CW, CW)
        scat[:, :, cols] = (
            mm(loc[...].reshape(S * n, K), expand[:, cols]).astype(BF).reshape(S, n, CW)
        )
    even = lax.rem(pl.program_id(0), 2) == 0

    @pl.when(even)
    def _():
        grad[...] = part[0].astype(F32) + part[1].astype(F32)

    @pl.when(jnp.logical_not(even))
    def _():
        grad[...] = jnp.sum(part[...].astype(F32), axis=0)


def on_device(contrast, incident, signs, adjoint, proj, mats, offsets, expand):
    any_spec = pl.BlockSpec(memory_space=pl.ANY)
    vmem = pl.BlockSpec(memory_space=pltpu.VMEM)
    smem = pl.BlockSpec(memory_space=pltpu.SMEM)
    dma = pltpu.SemaphoreType.DMA
    local, parts = pl.pallas_call(
        scatter_gradient_kernel,
        out_shape=(
            jax.ShapeDtypeStruct((S, NB, K), BF),
            jax.ShapeDtypeStruct((NZ, NB, GW), BF),
        ),
        in_specs=[smem, smem, any_spec, any_spec, any_spec, vmem, vmem, vmem],
        out_specs=(any_spec, any_spec),
        scratch_shapes=[
            pltpu.VMEM((NG, NB, GW), BF),
            pltpu.VMEM((S, NB, PTS), BF),
            pltpu.VMEM((S, NB, PTS), BF),
            pltpu.VMEM((NB + 2 * REACH, S, K), BF),
            pltpu.VMEM((REACH, S, K), BF),
            pltpu.VMEM((REACH, S, K), BF),
            pltpu.VMEM((S, NB, K), BF),
            pltpu.VMEM((NB, PTS), F32),
            pltpu.VMEM((NZ, 2, NB, GW), BF),
            pltpu.VMEM((2 * (NZ - 1), NB, GW), BF),
            pltpu.VMEM((NZ, NB, GW), BF),
            pltpu.VMEM((NB, GW), BF),
            pltpu.VMEM((ROWS, ROWS), BF),
            pltpu.VMEM((ROWS, ROWS), BF),
            pltpu.VMEM((ROWS, ROWS), BF),
            dma((NT,)),
            dma((NT,)),
            dma((4,)),
            dma((NCH, 2 * NZ - 1)),
            dma((NCH, 2 * NZ - 1)),
            dma((NT, NZ)),
            dma((NT, NZ)),
            dma((2,)),
            dma((2,)),
        ],
        compiler_params=pltpu.CompilerParams(
            collective_id=0, has_side_effects=True, vmem_limit_bytes=60 << 20
        ),
    )(signs[0], offsets, contrast, incident[0], adjoint[0], proj, mats, expand)

    scattered, gradient = pl.pallas_call(
        output_kernel,
        grid=(NT,),
        out_shape=(
            jax.ShapeDtypeStruct((S, NB, PTS), BF),
            jax.ShapeDtypeStruct((NB, GW), F32),
        ),
        in_specs=[
            pl.BlockSpec((S, TB, K), lambda i: (0, i, 0)),
            pl.BlockSpec((K, PTS), lambda i: (0, 0)),
            pl.BlockSpec((NZ, TB, GW), lambda i: (0, i, 0)),
        ],
        out_specs=(
            pl.BlockSpec((S, TB, PTS), lambda i: (0, i, 0)),
            pl.BlockSpec((TB, GW), lambda i: (i, 0)),
        ),
        compiler_params=pltpu.CompilerParams(vmem_limit_bytes=60 << 20),
    )(local, expand, parts)
    return scattered[None], gradient


def solution(mesh):
    in_specs = (
        P("tile", "group"),
        P("group", None, "tile", None),
        P("group", None, None),
        P("group", None, "tile", None),
        P(),
        P(),
        P(),
        P(),
    )
    out_specs = (P("group", None, "tile", None), P("tile", "group"))
    return jax.shard_map(
        on_device, mesh=mesh, in_specs=in_specs, out_specs=out_specs, check_vma=False
    )
```

```python
import jax
import jax.numpy as jnp
from jax import lax
from jax.experimental import pallas as pl
from jax.experimental.pallas import tpu as pltpu
from jax.sharding import PartitionSpec as P

MESH = pl.DeviceIdType.MESH
BF = jnp.bfloat16
F32 = jnp.float32

S = 8
K = 256
PTS = 1024
NB = 512
HB = 32
ROWS = S * HB
TB = 64
NT = NB // TB
NG = 8
GW = PTS // NG
CW = 256
NC = PTS // CW
REACH = 3
NZ = 4
ET = 2


def mm(a, b):
    return jnp.dot(a, b, preferred_element_type=F32)


def wait_bytes(ref, sem):
    pltpu.make_async_copy(ref, ref, sem).wait()


def scatter_gradient_kernel(
    signs_hbm, offsets_hbm, con_hbm, inc_hbm, adj_hbm, proj_hbm, mats_hbm, expand_hbm,
    loc_hbm, part_hbm,
    signs, offsets, proj, mats, expand,
    con_v, inc_v, adj_v, coef_v, low_v, high_v, loc_v, first_v, term_v, enc_points, enc_coeffs, perm,
    small_sem, in_sem, adj_sem, con_sem, loc_sem, own_sem,
    ag_send, ag_recv, rs_send, rs_recv, halo_send, halo_recv,
):
    g = lax.axis_index("group")
    tile = lax.axis_index("tile")
    last = lax.axis_size("tile") - 1

    def rows_of(t):
        return pl.ds(pl.multiple_of(t * TB, TB), TB)

    def inc_copy(t):
        r = rows_of(t)
        return pltpu.make_async_copy(inc_hbm.at[:, r], inc_v.at[:, r], in_sem.at[t])

    def adj_copy(t):
        r = rows_of(t)
        return pltpu.make_async_copy(adj_hbm.at[:, r], adj_v.at[:, r], adj_sem.at[t])

    con_copy = pltpu.make_async_copy(con_hbm, con_v.at[g], con_sem)
    small_copies = [
        pltpu.make_async_copy(src, dst, small_sem.at[i])
        for i, (src, dst) in enumerate(
            (
                (signs_hbm, signs),
                (offsets_hbm, offsets),
                (proj_hbm, proj),
                (mats_hbm, mats),
                (expand_hbm, expand),
            )
        )
    ]

    def gather(t, k):
        r = rows_of(t)
        return pltpu.make_async_remote_copy(
            src_ref=con_hbm.at[r],
            dst_ref=con_v.at[g, r],
            send_sem=ag_send,
            recv_sem=ag_recv.at[t],
            device_id=(lax.rem(g + k, NG), tile),
            device_id_type=MESH,
        )

    def rs_copy(t, k):
        peer = lax.rem(g + k, NG)
        return pltpu.make_async_remote_copy(
            src_ref=term_v.at[peer, rows_of(t)],
            dst_ref=part_hbm.at[g, rows_of(t)],
            send_sem=rs_send,
            recv_sem=rs_recv,
            device_id=(peer, tile),
            device_id_type=MESH,
        )

    def own_copy(t):
        r = rows_of(t)
        return pltpu.make_async_copy(term_v.at[g, r], part_hbm.at[g, r], own_sem)

    def loc_copy(t):
        r = rows_of(t)
        return pltpu.make_async_copy(loc_v.at[:, r], loc_hbm.at[:, r], loc_sem)

    def halo_up():
        return pltpu.make_async_remote_copy(
            src_ref=coef_v.at[pl.ds(NB, REACH)],
            dst_ref=low_v,
            send_sem=halo_send.at[0],
            recv_sem=halo_recv.at[0],
            device_id=(g, tile + 1),
            device_id_type=MESH,
        )

    def halo_down():
        return pltpu.make_async_remote_copy(
            src_ref=coef_v.at[pl.ds(REACH, REACH)],
            dst_ref=high_v,
            send_sem=halo_send.at[1],
            recv_sem=halo_recv.at[1],
            device_id=(g, tile - 1),
            device_id_type=MESH,
        )

    barrier = pltpu.get_barrier_semaphore()
    for k in range(1, NG):
        pl.semaphore_signal(
            barrier, inc=1, device_id=(lax.rem(g + k, NG), tile), device_id_type=MESH
        )
    for step_of in (1, last):
        pl.semaphore_signal(
            barrier, inc=1, device_id=(g, lax.rem(tile + step_of, last + 1)), device_id_type=MESH
        )

    small_copies[0].start()
    small_copies[1].start()
    for t in range(NT):
        inc_copy(t).start()
        adj_copy(t).start()
        if t == 1:
            con_copy.start()
            for copy in small_copies[2:]:
                copy.start()
    small_copies[0].wait()
    small_copies[1].wait()

    lane8 = lax.broadcasted_iota(jnp.int32, (S, ROWS), 1)
    row8 = lax.broadcasted_iota(jnp.int32, (S, ROWS), 0)
    sign = jnp.zeros((S, ROWS), F32)
    for e in range(S):
        for s in range(S):
            here = (row8 == e) & (lane8 // HB == s)
            sign = jnp.where(here, signs[e, s].astype(F32), sign)
    for b in range(0, HB, 2):
        pair = [jnp.where(lax.rem(lane8, HB) == b + i, sign, 0.0) for i in range(2)]
        enc_coeffs[pl.ds(b * S, 2 * S), :] = jnp.concatenate(pair, axis=0).astype(BF)
    lane = lax.broadcasted_iota(jnp.int32, (HB, ROWS), 1)
    row = lax.broadcasted_iota(jnp.int32, (HB, ROWS), 0)
    for e in range(S):
        wide = jnp.broadcast_to(sign[e : e + 1, :], (HB, ROWS))
        enc_points[pl.ds(e * HB, HB), :] = jnp.where(lax.rem(lane, HB) == row, wide, 0.0).astype(BF)
        there = (lane // S == row) & (lax.rem(lane, S) == e)
        perm[pl.ds(e * HB, HB), :] = jnp.where(there, 1.0, 0.0).astype(BF)

    def halves(t, tiles=1):
        for h in range(tiles * TB // HB):
            b0 = pl.multiple_of(t * TB + h * HB, HB)
            yield b0, pl.ds(b0, HB)

    def weighted(boxes, cols, field):
        adj = adj_v[:, boxes, cols].astype(F32)
        return jnp.sum(adj * field.reshape(S, HB, CW), axis=0)

    early = (2 * NZ - 1 - lax.rem(g, NZ) - NZ + (1 - g // NZ)) // 2

    def encode(i, carry):
        @pl.when(i == early)
        def _():
            pl.semaphore_wait(barrier, NG + 1)
            for t in range(NT):
                for k in range(1, NG):
                    gather(t, k).start()

        for t in range(ET):
            inc_copy(ET * i + t).wait()
            adj_copy(ET * i + t).wait()
        for b0, boxes in halves(ET * i, ET):
            for c in range(NC):
                cols = pl.ds(c * CW, CW)
                enc = mm(enc_points[...], inc_v[:, boxes, cols].reshape(ROWS, CW))
                first_v[boxes, cols] = weighted(boxes, cols, enc)
        return carry

    lax.fori_loop(0, NT // ET, encode, 0)
    con_copy.wait()
    for copy in small_copies[2:]:
        copy.wait()

    def project(t):
        sums = []
        for b0, boxes in halves(t):
            acc = jnp.zeros((ROWS, K), F32)
            for c in range(NC):
                cols = pl.ds(c * CW, CW)
                pieces = [con_v[c * (CW // GW) + q, boxes] for q in range(CW // GW)]
                src = inc_v[:, boxes, cols] * jnp.concatenate(pieces, axis=1)[None]
                acc = acc + mm(src.reshape(ROWS, CW), proj[cols, :])
            sums.append(acc.astype(BF))
        for (b0, boxes), acc in zip(halves(t), sums):
            coef = mm(enc_coeffs[...], acc).astype(BF)
            coef_v[pl.ds(b0 + REACH, HB)] = coef.reshape(HB, S, K)

    def expand_terms(t):
        sums = []
        for b0, boxes in halves(t):
            acc = jnp.zeros((ROWS, K), F32)
            for i in range(mats.shape[0]):
                moved = coef_v[pl.ds(b0 + REACH + offsets[i], HB)]
                acc = acc + mm(moved.reshape(ROWS, K), mats[i])
            sums.append(acc.astype(BF))
        locals_ = [mm(perm[...], acc).astype(BF) for acc in sums]
        for (b0, boxes), local in zip(halves(t), locals_):
            loc_v[:, boxes, :] = local.reshape(S, HB, K)
            for c in range(NC):
                cols = pl.ds(c * CW, CW)
                field = mm(local, expand[:, cols])
                term = (weighted(boxes, cols, field) + first_v[boxes, cols]).astype(BF)
                for q in range(CW // GW):
                    term_v[c * (CW // GW) + q, boxes, :] = term[:, q * GW : (q + 1) * GW]
        loc_copy(t).start()
        own_copy(t).start()
        for k in range(1, NG):
            rs_copy(t, k).start()

    def step(j, carry):
        @pl.when(j < NT)
        def _():
            wait_bytes(con_v.at[pl.ds(0, NG - 1), pl.ds(0, TB)], ag_recv.at[j])
            project(j)

        @pl.when((j == 1) & (tile > 0))
        def _():
            halo_down().start()

        @pl.when((j == NT - 1) & (tile < last))
        def _():
            halo_up().start()

        @pl.when(j == NT)
        def _():
            @pl.when(tile < last)
            def _():
                halo_down().wait_recv()
                coef_v[pl.ds(NB + REACH, REACH)] = high_v[...]

            @pl.when(tile == last)
            def _():
                coef_v[pl.ds(NB + REACH, REACH)] = jnp.zeros((REACH, S, K), BF)

        @pl.when(j == NT + 1)
        def _():
            @pl.when(tile > 0)
            def _():
                halo_up().wait_recv()
                coef_v[pl.ds(0, REACH)] = low_v[...]

            @pl.when(tile == 0)
            def _():
                coef_v[pl.ds(0, REACH)] = jnp.zeros((REACH, S, K), BF)

        @pl.when(j >= 2)
        def _():
            expand_terms(jnp.where(j == NT + 1, 0, j - 1))

        return carry

    lax.fori_loop(0, NT + 2, step, 0)

    wait_bytes(loc_v, loc_sem)
    wait_bytes(term_v.at[0], own_sem)
    wait_bytes(con_v.at[pl.ds(0, NG - 1)], ag_send)
    wait_bytes(term_v.at[pl.ds(0, NG - 1)], rs_send)
    wait_bytes(part_hbm.at[pl.ds(0, NG - 1)], rs_recv)

    @pl.when(tile < last)
    def _():
        halo_up().wait_send()

    @pl.when(tile > 0)
    def _():
        halo_down().wait_send()


def output_kernel(
    loc_hbm, expand_hbm, part_hbm, scat_hbm, grad_hbm,
    loc_v, expand, part_v, scat_v, grad_v, loc_sem, expand_sem, part_sem, scat_sem, grad_sem,
):
    def rows_of(t):
        return pl.ds(pl.multiple_of(t * TB, TB), TB)

    def loc_copy(t):
        r = rows_of(t)
        return pltpu.make_async_copy(loc_hbm.at[:, r], loc_v.at[:, r], loc_sem.at[t])

    def scat_copy(t, e):
        r = rows_of(t)
        return pltpu.make_async_copy(scat_v.at[e, r], scat_hbm.at[e, r], scat_sem)

    expand_copy = pltpu.make_async_copy(expand_hbm, expand, expand_sem)
    part_copy = pltpu.make_async_copy(part_hbm, part_v, part_sem)
    grad_copy = pltpu.make_async_copy(grad_v, grad_hbm, grad_sem)
    loc_copy(0).start()
    expand_copy.start()
    for t in range(1, NT):
        loc_copy(t).start()
    part_copy.start()
    expand_copy.wait()

    def step(t, carry):
        loc_copy(t).wait()
        r = rows_of(t)
        rows = loc_v[:, r, :].reshape(S * TB, K)
        for c in range(NC):
            cols = pl.ds(c * CW, CW)
            scat_v[:, r, cols] = mm(rows, expand[:, cols]).astype(BF).reshape(S, TB, CW)
        for e in range(S):
            scat_copy(t, e).start()

        @pl.when(t == NT - 2)
        def _():
            part_copy.wait()
            grad_v[...] = jnp.sum(part_v[...].astype(F32), axis=0)
            grad_copy.start()

        return carry

    lax.fori_loop(0, NT, step, 0)
    wait_bytes(scat_v, scat_sem)
    grad_copy.wait()


def on_device(contrast, incident, signs, adjoint, proj, mats, offsets, expand):
    any_spec = pl.BlockSpec(memory_space=pl.ANY)
    dma = pltpu.SemaphoreType.DMA
    local, parts = pl.pallas_call(
        scatter_gradient_kernel,
        out_shape=(
            jax.ShapeDtypeStruct((S, NB, K), BF),
            jax.ShapeDtypeStruct((NG, NB, GW), BF),
        ),
        in_specs=[any_spec] * 8,
        out_specs=(any_spec, any_spec),
        scratch_shapes=[
            pltpu.SMEM((S, S), jnp.int32),
            pltpu.SMEM(offsets.shape, jnp.int32),
            pltpu.VMEM(proj.shape, BF),
            pltpu.VMEM(mats.shape, BF),
            pltpu.VMEM(expand.shape, BF),
            pltpu.VMEM((NG, NB, GW), BF),
            pltpu.VMEM((S, NB, PTS), BF),
            pltpu.VMEM((S, NB, PTS), BF),
            pltpu.VMEM((NB + 2 * REACH, S, K), BF),
            pltpu.VMEM((REACH, S, K), BF),
            pltpu.VMEM((REACH, S, K), BF),
            pltpu.VMEM((S, NB, K), BF),
            pltpu.VMEM((NB, PTS), F32),
            pltpu.VMEM((NG, NB, GW), BF),
            pltpu.VMEM((ROWS, ROWS), BF),
            pltpu.VMEM((ROWS, ROWS), BF),
            pltpu.VMEM((ROWS, ROWS), BF),
            dma((5,)),
            dma((NT,)),
            dma((NT,)),
            dma,
            dma,
            dma,
            dma,
            dma((NT,)),
            dma,
            dma,
            dma((2,)),
            dma((2,)),
        ],
        compiler_params=pltpu.CompilerParams(
            collective_id=0, has_side_effects=True, vmem_limit_bytes=60 << 20
        ),
    )(signs[0], offsets, contrast, incident[0], adjoint[0], proj, mats, expand)

    scattered, gradient = pl.pallas_call(
        output_kernel,
        out_shape=(
            jax.ShapeDtypeStruct((S, NB, PTS), BF),
            jax.ShapeDtypeStruct((NB, GW), F32),
        ),
        in_specs=[any_spec] * 3,
        out_specs=(any_spec, any_spec),
        scratch_shapes=[
            pltpu.VMEM((S, NB, K), BF),
            pltpu.VMEM(expand.shape, BF),
            pltpu.VMEM((NG, NB, GW), BF),
            pltpu.VMEM((S, NB, PTS), BF),
            pltpu.VMEM((NB, GW), F32),
            dma((NT,)),
            dma,
            dma,
            dma,
            dma,
        ],
        compiler_params=pltpu.CompilerParams(vmem_limit_bytes=60 << 20),
    )(local, expand, parts)
    return scattered[None], gradient


def solution(mesh):
    in_specs = (
        P("tile", "group"),
        P("group", None, "tile", None),
        P("group", None, None),
        P("group", None, "tile", None),
        P(),
        P(),
        P(),
        P(),
    )
    out_specs = (P("group", None, "tile", None), P("tile", "group"))
    return jax.shard_map(
        on_device, mesh=mesh, in_specs=in_specs, out_specs=out_specs, check_vma=False
    )
```

```python
import jax
import jax.numpy as jnp
from jax import lax
from jax.experimental import pallas as pl
from jax.experimental.pallas import tpu as pltpu
from jax.sharding import PartitionSpec as P

MESH = pl.DeviceIdType.MESH
BF = jnp.bfloat16
F32 = jnp.float32

S = 8
K = 256
PTS = 1024
NB = 512
HB = 32
ROWS = S * HB
TB = 64
NT = NB // TB
NG = 8
GW = PTS // NG
CW = 256
NC = PTS // CW
REACH = 3
LANES = 128
NZ = 4
PEERS = [(1, 2), (1, 1), (1, 3), (0, 2), (1, 0), (0, 1), (0, 3)]
ET = 2


def mm(a, b):
    return jnp.dot(a, b, preferred_element_type=F32)


def wait_bytes(ref, sem):
    pltpu.make_async_copy(ref, ref, sem).wait()


def scatter_gradient_kernel(
    signs_hbm, offsets_hbm, con_hbm, inc_hbm, adj_hbm, proj_hbm, mats_hbm, expand_hbm,
    loc_hbm, part_hbm,
    signs, offsets, proj, mats, expand,
    con_v, inc_v, adj_v, coef_v, low_v, high_v, loc_v, first_v, term_v, enc_points, enc_coeffs,
    small_sem, in_sem, adj_sem, con_sem, loc_sem, own_sem,
    ag_send, ag_recv, rs_send, rs_recv, halo_send, halo_recv,
):
    g = lax.axis_index("group")
    tile = lax.axis_index("tile")
    last = lax.axis_size("tile") - 1

    flip = lax.rem(tile, 2)

    def peer_at(k):
        dy, dz = PEERS[k - 1]
        step = dz + flip * ((NZ - 2 * dz) if dz else 0)
        return lax.rem(g // NZ + dy, 2) * NZ + lax.rem(g + step, NZ)

    def rows_of(t):
        return pl.ds(pl.multiple_of(t * TB, TB), TB)

    def inc_copy(t):
        r = rows_of(t)
        return pltpu.make_async_copy(inc_hbm.at[:, r], inc_v.at[:, r], in_sem.at[t])

    def adj_copy(t):
        r = rows_of(t)
        return pltpu.make_async_copy(adj_hbm.at[:, r], adj_v.at[:, r], adj_sem.at[t])

    con_copy = pltpu.make_async_copy(con_hbm, con_v.at[g], con_sem)
    small_copies = [
        pltpu.make_async_copy(src, dst, small_sem.at[i])
        for i, (src, dst) in enumerate(
            (
                (signs_hbm, signs),
                (offsets_hbm, offsets),
                (proj_hbm, proj),
                (mats_hbm, mats),
                (expand_hbm, expand),
            )
        )
    ]

    def gather(t, k):
        r = rows_of(t)
        return pltpu.make_async_remote_copy(
            src_ref=con_hbm.at[r],
            dst_ref=con_v.at[g, r],
            send_sem=ag_send,
            recv_sem=ag_recv.at[t],
            device_id=(peer_at(k), tile),
            device_id_type=MESH,
        )

    def rs_copy(t, k):
        peer = peer_at(k)
        return pltpu.make_async_remote_copy(
            src_ref=term_v.at[peer, rows_of(t)],
            dst_ref=part_hbm.at[g, rows_of(t)],
            send_sem=rs_send,
            recv_sem=rs_recv,
            device_id=(peer, tile),
            device_id_type=MESH,
        )

    def own_copy(t):
        r = rows_of(t)
        return pltpu.make_async_copy(term_v.at[g, r], part_hbm.at[g, r], own_sem)

    def loc_copy(t):
        r = rows_of(t)
        return pltpu.make_async_copy(loc_v.at[:, r], loc_hbm.at[:, r], loc_sem)

    def halo_up():
        return pltpu.make_async_remote_copy(
            src_ref=coef_v.at[:, pl.ds(NB * S, REACH * S)],
            dst_ref=low_v,
            send_sem=halo_send.at[0],
            recv_sem=halo_recv.at[0],
            device_id=(g, tile + 1),
            device_id_type=MESH,
        )

    def halo_down():
        return pltpu.make_async_remote_copy(
            src_ref=coef_v.at[:, pl.ds(REACH * S, REACH * S)],
            dst_ref=high_v,
            send_sem=halo_send.at[1],
            recv_sem=halo_recv.at[1],
            device_id=(g, tile - 1),
            device_id_type=MESH,
        )

    barrier = pltpu.get_barrier_semaphore()
    for k in range(1, NG):
        pl.semaphore_signal(
            barrier, inc=1, device_id=(lax.rem(g + k, NG), tile), device_id_type=MESH
        )
    for step_of in (1, last):
        pl.semaphore_signal(
            barrier, inc=1, device_id=(g, lax.rem(tile + step_of, last + 1)), device_id_type=MESH
        )

    small_copies[0].start()
    small_copies[1].start()
    for t in range(NT):
        inc_copy(t).start()
        adj_copy(t).start()
        if t == 1:
            con_copy.start()
            for copy in small_copies[2:]:
                copy.start()
    small_copies[0].wait()
    small_copies[1].wait()

    lane8 = lax.broadcasted_iota(jnp.int32, (S, ROWS), 1)
    row8 = lax.broadcasted_iota(jnp.int32, (S, ROWS), 0)
    sign = jnp.zeros((S, ROWS), F32)
    for e in range(S):
        for s in range(S):
            here = (row8 == e) & (lane8 // HB == s)
            sign = jnp.where(here, signs[e, s].astype(F32), sign)
    for b in range(0, HB, 2):
        pair = [jnp.where(lax.rem(lane8, HB) == b + i, sign, 0.0) for i in range(2)]
        enc_coeffs[pl.ds(b * S, 2 * S), :] = jnp.concatenate(pair, axis=0).astype(BF)
    lane = lax.broadcasted_iota(jnp.int32, (HB, ROWS), 1)
    row = lax.broadcasted_iota(jnp.int32, (HB, ROWS), 0)
    for e in range(S):
        wide = jnp.broadcast_to(sign[e : e + 1, :], (HB, ROWS))
        enc_points[pl.ds(e * HB, HB), :] = jnp.where(lax.rem(lane, HB) == row, wide, 0.0).astype(BF)

    def halves(t, tiles=1):
        for h in range(tiles * TB // HB):
            b0 = pl.multiple_of(t * TB + h * HB, HB)
            yield b0, pl.ds(b0, HB)

    def weighted(boxes, cols, field):
        adj = adj_v[:, boxes, cols].astype(F32)
        return jnp.sum(adj * field.reshape(S, HB, CW), axis=0)

    early = (2 * NZ - 1 - lax.rem(g, NZ) - NZ + (1 - g // NZ)) // 2

    def encode(i, carry):
        @pl.when(i == early)
        def _():
            pl.semaphore_wait(barrier, NG + 1)
            for t in range(NT):
                for k in range(1, NG):
                    gather(t, k).start()

        for t in range(ET):
            inc_copy(ET * i + t).wait()
            adj_copy(ET * i + t).wait()
        for b0, boxes in halves(ET * i, ET):
            for c in range(NC):
                cols = pl.ds(c * CW, CW)
                enc = mm(enc_points[...], inc_v[:, boxes, cols].reshape(ROWS, CW))
                first_v[boxes, cols] = weighted(boxes, cols, enc)
        return carry

    lax.fori_loop(0, NT // ET, encode, 0)
    con_copy.wait()
    for copy in small_copies[2:]:
        copy.wait()

    def project(t):
        sums = []
        for b0, boxes in halves(t):
            acc = jnp.zeros((ROWS, K), F32)
            for c in range(NC):
                cols = pl.ds(c * CW, CW)
                pieces = [con_v[c * (CW // GW) + q, boxes] for q in range(CW // GW)]
                src = inc_v[:, boxes, cols] * jnp.concatenate(pieces, axis=1)[None]
                acc = acc + mm(src.reshape(ROWS, CW), proj[cols, :])
            sums.append(acc.astype(BF))
        for (b0, boxes), acc in zip(halves(t), sums):
            coef = mm(enc_coeffs[...], acc)
            to = pl.ds(pl.multiple_of((b0 + REACH) * S, S), ROWS)
            for w in range(K // LANES):
                coef_v[w, to, :] = coef[:, w * LANES : (w + 1) * LANES]

    def expand_terms(t):
        sums = []
        for b0, boxes in halves(t):
            acc = jnp.zeros((ROWS, K), F32)
            for i in range(mats.shape[0]):
                first = (b0 + REACH + offsets[i]) * S
                moved = [
                    jnp.concatenate(
                        [coef_v[w, pl.ds(first + e, HB, stride=S), :] for e in range(S)], axis=0
                    ).astype(BF)
                    for w in range(K // LANES)
                ]
                acc = acc + mm(jnp.concatenate(moved, axis=1), mats[i])
            sums.append(acc.astype(BF))
        for (b0, boxes), local in zip(halves(t), sums):
            loc_v[:, boxes, :] = local.reshape(S, HB, K)
            for c in range(NC):
                cols = pl.ds(c * CW, CW)
                field = mm(local, expand[:, cols])
                term = (weighted(boxes, cols, field) + first_v[boxes, cols]).astype(BF)
                for q in range(CW // GW):
                    term_v[c * (CW // GW) + q, boxes, :] = term[:, q * GW : (q + 1) * GW]
        loc_copy(t).start()
        own_copy(t).start()
        for k in range(1, NG):
            rs_copy(t, k).start()

    def step(j, carry):
        @pl.when(j < NT)
        def _():
            wait_bytes(con_v.at[pl.ds(0, NG - 1), pl.ds(0, TB)], ag_recv.at[j])
            project(j)

        @pl.when((j == 1) & (tile > 0))
        def _():
            halo_down().start()

        @pl.when((j == NT - 1) & (tile < last))
        def _():
            halo_up().start()

        @pl.when(j == NT)
        def _():
            @pl.when(tile < last)
            def _():
                halo_down().wait_recv()
                coef_v[:, pl.ds((NB + REACH) * S, REACH * S)] = high_v[...]

            @pl.when(tile == last)
            def _():
                coef_v[:, pl.ds((NB + REACH) * S, REACH * S)] = jnp.zeros((K // LANES, REACH * S, LANES), F32)

        @pl.when(j == NT + 1)
        def _():
            @pl.when(tile > 0)
            def _():
                halo_up().wait_recv()
                coef_v[:, pl.ds(0, REACH * S)] = low_v[...]

            @pl.when(tile == 0)
            def _():
                coef_v[:, pl.ds(0, REACH * S)] = jnp.zeros((K // LANES, REACH * S, LANES), F32)

        @pl.when(j >= 2)
        def _():
            expand_terms(jnp.where(j == NT + 1, 0, j - 1))

        return carry

    lax.fori_loop(0, NT + 2, step, 0)

    wait_bytes(loc_v, loc_sem)
    wait_bytes(term_v.at[0], own_sem)
    wait_bytes(con_v.at[pl.ds(0, NG - 1)], ag_send)
    wait_bytes(term_v.at[pl.ds(0, NG - 1)], rs_send)
    wait_bytes(part_hbm.at[pl.ds(0, NG - 1)], rs_recv)

    @pl.when(tile < last)
    def _():
        halo_up().wait_send()

    @pl.when(tile > 0)
    def _():
        halo_down().wait_send()


def output_kernel(
    loc_hbm, expand_hbm, part_hbm, scat_hbm, grad_hbm,
    loc_v, expand, part_v, scat_v, grad_v, loc_sem, expand_sem, part_sem, scat_sem, grad_sem,
):
    def rows_of(t):
        return pl.ds(pl.multiple_of(t * TB, TB), TB)

    def loc_copy(t):
        r = rows_of(t)
        return pltpu.make_async_copy(loc_hbm.at[:, r], loc_v.at[:, r], loc_sem.at[t])

    def scat_copy(t, e):
        r = rows_of(t)
        return pltpu.make_async_copy(scat_v.at[e, r], scat_hbm.at[e, r], scat_sem)

    expand_copy = pltpu.make_async_copy(expand_hbm, expand, expand_sem)
    part_copy = pltpu.make_async_copy(part_hbm, part_v, part_sem)
    grad_copy = pltpu.make_async_copy(grad_v, grad_hbm, grad_sem)
    loc_copy(0).start()
    expand_copy.start()
    for t in range(1, NT):
        loc_copy(t).start()
    part_copy.start()
    expand_copy.wait()

    def step(i, carry):
        tiles = [ET * i + t for t in range(ET)]
        for t in tiles:
            loc_copy(t).wait()
        for t in tiles:
            r = rows_of(t)
            rows = loc_v[:, r, :].reshape(S * TB, K)
            for c in range(NC):
                cols = pl.ds(c * CW, CW)
                scat_v[:, r, cols] = mm(rows, expand[:, cols]).astype(BF).reshape(S, TB, CW)
        for t in tiles:
            for e in range(S):
                scat_copy(t, e).start()

        @pl.when(i == NT // ET - 2)
        def _():
            part_copy.wait()
            grad_v[...] = jnp.sum(part_v[...].astype(F32), axis=0)
            grad_copy.start()

        return carry

    lax.fori_loop(0, NT // ET, step, 0)
    wait_bytes(scat_v, scat_sem)
    grad_copy.wait()


def on_device(contrast, incident, signs, adjoint, proj, mats, offsets, expand):
    any_spec = pl.BlockSpec(memory_space=pl.ANY)
    dma = pltpu.SemaphoreType.DMA
    local, parts = pl.pallas_call(
        scatter_gradient_kernel,
        out_shape=(
            jax.ShapeDtypeStruct((S, NB, K), BF),
            jax.ShapeDtypeStruct((NG, NB, GW), BF),
        ),
        in_specs=[any_spec] * 8,
        out_specs=(any_spec, any_spec),
        scratch_shapes=[
            pltpu.SMEM((S, S), jnp.int32),
            pltpu.SMEM(offsets.shape, jnp.int32),
            pltpu.VMEM(proj.shape, BF),
            pltpu.VMEM(mats.shape, BF),
            pltpu.VMEM(expand.shape, BF),
            pltpu.VMEM((NG, NB, GW), BF),
            pltpu.VMEM((S, NB, PTS), BF),
            pltpu.VMEM((S, NB, PTS), BF),
            pltpu.VMEM((K // LANES, (NB + 2 * REACH) * S, LANES), F32),
            pltpu.VMEM((K // LANES, REACH * S, LANES), F32),
            pltpu.VMEM((K // LANES, REACH * S, LANES), F32),
            pltpu.VMEM((S, NB, K), BF),
            pltpu.VMEM((NB, PTS), F32),
            pltpu.VMEM((NG, NB, GW), BF),
            pltpu.VMEM((ROWS, ROWS), BF),
            pltpu.VMEM((ROWS, ROWS), BF),
            dma((5,)),
            dma((NT,)),
            dma((NT,)),
            dma,
            dma,
            dma,
            dma,
            dma((NT,)),
            dma,
            dma,
            dma((2,)),
            dma((2,)),
        ],
        compiler_params=pltpu.CompilerParams(
            collective_id=0, has_side_effects=True, vmem_limit_bytes=60 << 20
        ),
    )(signs[0], offsets, contrast, incident[0], adjoint[0], proj, mats, expand)

    scattered, gradient = pl.pallas_call(
        output_kernel,
        out_shape=(
            jax.ShapeDtypeStruct((S, NB, PTS), BF),
            jax.ShapeDtypeStruct((NB, GW), F32),
        ),
        in_specs=[any_spec] * 3,
        out_specs=(any_spec, any_spec),
        scratch_shapes=[
            pltpu.VMEM((S, NB, K), BF),
            pltpu.VMEM(expand.shape, BF),
            pltpu.VMEM((NG, NB, GW), BF),
            pltpu.VMEM((S, NB, PTS), BF),
            pltpu.VMEM((NB, GW), F32),
            dma((NT,)),
            dma,
            dma,
            dma,
            dma,
        ],
        compiler_params=pltpu.CompilerParams(vmem_limit_bytes=60 << 20),
    )(local, expand, parts)
    return scattered[None], gradient


def solution(mesh):
    in_specs = (
        P("tile", "group"),
        P("group", None, "tile", None),
        P("group", None, None),
        P("group", None, "tile", None),
        P(),
        P(),
        P(),
        P(),
    )
    out_specs = (P("group", None, "tile", None), P("tile", "group"))
    return jax.shard_map(
        on_device, mesh=mesh, in_specs=in_specs, out_specs=out_specs, check_vma=False
    )
```

```python
import jax
import jax.numpy as jnp
from jax import lax
from jax.experimental import pallas as pl
from jax.experimental.pallas import tpu as pltpu
from jax.sharding import PartitionSpec as P

MESH = pl.DeviceIdType.MESH
BF = jnp.bfloat16
F32 = jnp.float32

S = 8
K = 256
PTS = 1024
NB = 512
HB = 32
ROWS = S * HB
TB = 64
NT = NB // TB
NG = 8
GW = PTS // NG
CW = 256
NC = PTS // CW
REACH = 3
LANES = 128
NZ = 4
PEERS = [(1, 2), (1, 1), (1, 3), (0, 2), (1, 0), (0, 1), (0, 3)]
HP = 1
ET = 2


def mm(a, b):
    return jnp.dot(a, b, preferred_element_type=F32)


def wait_bytes(ref, sem):
    pltpu.make_async_copy(ref, ref, sem).wait()


def scatter_gradient_kernel(
    signs_hbm, offsets_hbm, con_hbm, inc_hbm, adj_hbm, proj_hbm, mats_hbm, expand_hbm,
    loc_hbm, part_hbm, ready_hbm,
    signs, offsets, proj, mats, expand,
    con_v, inc_v, adj_v, coef_v, low_v, high_v, loc_v, first_v, term_v, enc_points, enc_coeffs,
    small_sem, in_sem, adj_sem, con_sem, loc_sem, own_sem, ready_sem,
    ag_send, ag_recv, rs_send, rs_recv, halo_send, halo_recv,
):
    g = lax.axis_index("group")
    tile = lax.axis_index("tile")
    last = lax.axis_size("tile") - 1

    flip = lax.rem(tile, 2)

    def peer_at(k):
        dy, dz = PEERS[k - 1]
        step = dz + flip * ((NZ - 2 * dz) if dz else 0)
        return lax.rem(g // NZ + dy, 2) * NZ + lax.rem(g + step, NZ)

    def rows_of(t):
        return pl.ds(pl.multiple_of(t * TB, TB), TB)

    def inc_copy(t):
        r = rows_of(t)
        return pltpu.make_async_copy(inc_hbm.at[:, r], inc_v.at[:, r], in_sem.at[t])

    def adj_copy(t):
        r = rows_of(t)
        return pltpu.make_async_copy(adj_hbm.at[:, r], adj_v.at[:, r], adj_sem.at[t])

    con_copy = pltpu.make_async_copy(con_hbm, con_v.at[g], con_sem)
    small_copies = [
        pltpu.make_async_copy(src, dst, small_sem.at[i])
        for i, (src, dst) in enumerate(
            (
                (signs_hbm, signs),
                (offsets_hbm, offsets),
                (proj_hbm, proj),
                (mats_hbm, mats),
                (expand_hbm, expand),
            )
        )
    ]

    def gather(t, k):
        r = rows_of(t)
        return pltpu.make_async_remote_copy(
            src_ref=con_hbm.at[r],
            dst_ref=con_v.at[g, r],
            send_sem=ag_send,
            recv_sem=ag_recv.at[t],
            device_id=(peer_at(k), tile),
            device_id_type=MESH,
        )

    def rs_copy(t, k):
        peer = peer_at(k)
        return pltpu.make_async_remote_copy(
            src_ref=term_v.at[peer, rows_of(t)],
            dst_ref=part_hbm.at[g, rows_of(t)],
            send_sem=rs_send,
            recv_sem=rs_recv,
            device_id=(peer, tile),
            device_id_type=MESH,
        )

    def own_copy(t):
        r = rows_of(t)
        return pltpu.make_async_copy(term_v.at[g, r], part_hbm.at[g, r], own_sem)

    def loc_copy(t):
        r = rows_of(t)
        return pltpu.make_async_copy(loc_v.at[:, r], loc_hbm.at[:, r], loc_sem)

    def ready_copy(t):
        to = pl.ds(pl.multiple_of((t - ET) * TB, TB), TB)
        return pltpu.make_async_copy(inc_v.at[:, rows_of(t)], ready_hbm.at[:, to], ready_sem)

    def halo_up():
        return pltpu.make_async_remote_copy(
            src_ref=coef_v.at[:, pl.ds(NB * S, REACH * S)],
            dst_ref=low_v,
            send_sem=halo_send.at[0],
            recv_sem=halo_recv.at[0],
            device_id=(g, tile + 1),
            device_id_type=MESH,
        )

    def halo_down():
        return pltpu.make_async_remote_copy(
            src_ref=coef_v.at[:, pl.ds(REACH * S, REACH * S)],
            dst_ref=high_v,
            send_sem=halo_send.at[1],
            recv_sem=halo_recv.at[1],
            device_id=(g, tile - 1),
            device_id_type=MESH,
        )

    barrier = pltpu.get_barrier_semaphore()
    for k in range(1, NG):
        pl.semaphore_signal(
            barrier, inc=1, device_id=(lax.rem(g + k, NG), tile), device_id_type=MESH
        )
    for step_of in (1, last):
        pl.semaphore_signal(
            barrier, inc=1, device_id=(g, lax.rem(tile + step_of, last + 1)), device_id_type=MESH
        )

    small_copies[0].start()
    small_copies[1].start()
    for t in range(NT):
        inc_copy(t).start()
        adj_copy(t).start()
        if t == 1:
            con_copy.start()
            for copy in small_copies[2:]:
                copy.start()
    small_copies[0].wait()
    small_copies[1].wait()

    lane8 = lax.broadcasted_iota(jnp.int32, (S, ROWS), 1)
    row8 = lax.broadcasted_iota(jnp.int32, (S, ROWS), 0)
    sign = jnp.zeros((S, ROWS), F32)
    for e in range(S):
        for s in range(S):
            here = (row8 == e) & (lane8 // HB == s)
            sign = jnp.where(here, signs[e, s].astype(F32), sign)
    for b in range(0, HB, 2):
        pair = [jnp.where(lax.rem(lane8, HB) == b + i, sign, 0.0) for i in range(2)]
        enc_coeffs[pl.ds(b * S, 2 * S), :] = jnp.concatenate(pair, axis=0).astype(BF)
    lane = lax.broadcasted_iota(jnp.int32, (HB, ROWS), 1)
    row = lax.broadcasted_iota(jnp.int32, (HB, ROWS), 0)
    for e in range(S):
        wide = jnp.broadcast_to(sign[e : e + 1, :], (HB, ROWS))
        enc_points[pl.ds(e * HB, HB), :] = jnp.where(lax.rem(lane, HB) == row, wide, 0.0).astype(BF)

    def halves(t, tiles=1):
        for h in range(tiles * TB // HB):
            b0 = pl.multiple_of(t * TB + h * HB, HB)
            yield b0, pl.ds(b0, HB)

    def weighted(boxes, cols, field):
        adj = adj_v[:, boxes, cols].astype(F32)
        return jnp.sum(adj * field.reshape(S, HB, CW), axis=0)

    early = (2 * NZ - 1 - lax.rem(g, NZ) - NZ + (1 - g // NZ)) // 2

    def encode(i, carry):
        @pl.when(i == early)
        def _():
            pl.semaphore_wait(barrier, NG + 1)
            for t in range(NT):
                for k in range(1, NG):
                    gather(t, k).start()

        for t in range(ET):
            inc_copy(ET * i + t).wait()
            adj_copy(ET * i + t).wait()
        for b0, boxes in halves(ET * i, ET):
            for c in range(NC):
                cols = pl.ds(c * CW, CW)
                enc = mm(enc_points[...], inc_v[:, boxes, cols].reshape(ROWS, CW))
                first_v[boxes, cols] = weighted(boxes, cols, enc)
        return carry

    lax.fori_loop(0, NT // ET, encode, 0)
    con_copy.wait()
    for copy in small_copies[2:]:
        copy.wait()

    def project(t):
        sums = []
        for b0, boxes in halves(t):
            acc = jnp.zeros((ROWS, K), F32)
            for c in range(NC):
                cols = pl.ds(c * CW, CW)
                pieces = [con_v[c * (CW // GW) + q, boxes] for q in range(CW // GW)]
                src = inc_v[:, boxes, cols] * jnp.concatenate(pieces, axis=1)[None]
                acc = acc + mm(src.reshape(ROWS, CW), proj[cols, :])
            sums.append(acc.astype(BF))
        for (b0, boxes), acc in zip(halves(t), sums):
            coef = mm(enc_coeffs[...], acc)
            to = pl.ds(pl.multiple_of((b0 + REACH) * S, S), ROWS)
            for w in range(K // LANES):
                coef_v[w, to, :] = coef[:, w * LANES : (w + 1) * LANES]

    def expand_terms(t):
        sums = []
        for b0, boxes in halves(t):
            acc = jnp.zeros((ROWS, K), F32)
            for i in range(mats.shape[0]):
                first = (b0 + REACH + offsets[i]) * S
                moved = [
                    jnp.concatenate(
                        [coef_v[w, pl.ds(first + e, HB, stride=S), :] for e in range(S)], axis=0
                    ).astype(BF)
                    for w in range(K // LANES)
                ]
                acc = acc + mm(jnp.concatenate(moved, axis=1), mats[i])
            sums.append(acc.astype(BF))
        for (b0, boxes), local in zip(halves(t), sums):
            loc_v[:, boxes, :] = local.reshape(S, HB, K)
            for c in range(NC):
                cols = pl.ds(c * CW, CW)
                field = mm(local, expand[:, cols])
                inc_v[:, boxes, cols] = field.astype(BF).reshape(S, HB, CW)
                term = (weighted(boxes, cols, field) + first_v[boxes, cols]).astype(BF)
                for q in range(CW // GW):
                    term_v[c * (CW // GW) + q, boxes, :] = term[:, q * GW : (q + 1) * GW]
        loc_copy(t).start()
        own_copy(t).start()

        @pl.when((t >= ET) & (t < ET * (1 + HP)))
        def _():
            ready_copy(t).start()

        for k in range(1, NG):
            rs_copy(t, k).start()

    def step(j, carry):
        @pl.when(j < NT)
        def _():
            wait_bytes(con_v.at[pl.ds(0, NG - 1), pl.ds(0, TB)], ag_recv.at[j])
            project(j)

        @pl.when((j == 1) & (tile > 0))
        def _():
            halo_down().start()

        @pl.when((j == NT - 1) & (tile < last))
        def _():
            halo_up().start()

        @pl.when(j == NT)
        def _():
            @pl.when(tile < last)
            def _():
                halo_down().wait_recv()
                coef_v[:, pl.ds((NB + REACH) * S, REACH * S)] = high_v[...]

            @pl.when(tile == last)
            def _():
                coef_v[:, pl.ds((NB + REACH) * S, REACH * S)] = jnp.zeros((K // LANES, REACH * S, LANES), F32)

        @pl.when(j == NT + 1)
        def _():
            @pl.when(tile > 0)
            def _():
                halo_up().wait_recv()
                coef_v[:, pl.ds(0, REACH * S)] = low_v[...]

            @pl.when(tile == 0)
            def _():
                coef_v[:, pl.ds(0, REACH * S)] = jnp.zeros((K // LANES, REACH * S, LANES), F32)

        @pl.when(j >= 2)
        def _():
            expand_terms(jnp.where(j == NT + 1, 0, j - 1))

        return carry

    lax.fori_loop(0, NT + 2, step, 0)

    wait_bytes(loc_v, loc_sem)
    wait_bytes(ready_hbm, ready_sem)
    wait_bytes(term_v.at[0], own_sem)
    wait_bytes(con_v.at[pl.ds(0, NG - 1)], ag_send)
    wait_bytes(term_v.at[pl.ds(0, NG - 1)], rs_send)
    wait_bytes(part_hbm.at[pl.ds(0, NG - 1)], rs_recv)

    @pl.when(tile < last)
    def _():
        halo_up().wait_send()

    @pl.when(tile > 0)
    def _():
        halo_down().wait_send()


def output_kernel(
    loc_hbm, expand_hbm, part_hbm, ready_hbm, scat_hbm, grad_hbm,
    loc_v, expand, part_v, scat_v, grad_v,
    loc_sem, expand_sem, part_sem, ready_sem, scat_sem, grad_sem,
):
    def rows_of(t):
        return pl.ds(pl.multiple_of(t * TB, TB), TB)

    def loc_copy(t):
        r = rows_of(t)
        return pltpu.make_async_copy(loc_hbm.at[:, r], loc_v.at[:, r], loc_sem.at[t])

    def scat_copy(t, e):
        r = rows_of(t)
        return pltpu.make_async_copy(scat_v.at[e, r], scat_hbm.at[e, r], scat_sem)

    def ready_copy(t):
        src = ready_hbm.at[:, (t - ET) * TB : (t - ET + 1) * TB]
        return pltpu.make_async_copy(src, scat_v.at[:, rows_of(t)], ready_sem.at[t - ET])

    expand_copy = pltpu.make_async_copy(expand_hbm, expand, expand_sem)
    part_copy = pltpu.make_async_copy(part_hbm, part_v, part_sem)
    grad_copy = pltpu.make_async_copy(grad_v, grad_hbm, grad_sem)
    loc_copy(0).start()
    expand_copy.start()
    loc_copy(1).start()
    for t in range(ET, ET * (1 + HP)):
        ready_copy(t).start()
    for t in range(ET * (1 + HP), NT):
        loc_copy(t).start()
    part_copy.start()
    expand_copy.wait()

    def step(i, carry):
        tiles = [ET * jnp.where(i == 0, 0, i + HP) + t for t in range(ET)]
        for t in tiles:
            loc_copy(t).wait()
        for t in tiles:
            r = rows_of(t)
            rows = loc_v[:, r, :].reshape(S * TB, K)
            for c in range(NC):
                cols = pl.ds(c * CW, CW)
                scat_v[:, r, cols] = mm(rows, expand[:, cols]).astype(BF).reshape(S, TB, CW)
        for t in tiles:
            for e in range(S):
                scat_copy(t, e).start()

        @pl.when(i == 0)
        def _():
            for t in range(ET, ET * (1 + HP)):
                ready_copy(t).wait()
                for e in range(S):
                    scat_copy(t, e).start()

        @pl.when(i == NT // ET - HP - 2)
        def _():
            part_copy.wait()
            grad_v[...] = jnp.sum(part_v[...].astype(F32), axis=0)
            grad_copy.start()

        return carry

    lax.fori_loop(0, NT // ET - HP, step, 0)
    wait_bytes(scat_v, scat_sem)
    grad_copy.wait()


def on_device(contrast, incident, signs, adjoint, proj, mats, offsets, expand):
    any_spec = pl.BlockSpec(memory_space=pl.ANY)
    dma = pltpu.SemaphoreType.DMA
    local, parts, ready = pl.pallas_call(
        scatter_gradient_kernel,
        out_shape=(
            jax.ShapeDtypeStruct((S, NB, K), BF),
            jax.ShapeDtypeStruct((NG, NB, GW), BF),
            jax.ShapeDtypeStruct((S, HP * ET * TB, PTS), BF),
        ),
        in_specs=[any_spec] * 8,
        out_specs=(any_spec,) * 3,
        scratch_shapes=[
            pltpu.SMEM((S, S), jnp.int32),
            pltpu.SMEM(offsets.shape, jnp.int32),
            pltpu.VMEM(proj.shape, BF),
            pltpu.VMEM(mats.shape, BF),
            pltpu.VMEM(expand.shape, BF),
            pltpu.VMEM((NG, NB, GW), BF),
            pltpu.VMEM((S, NB, PTS), BF),
            pltpu.VMEM((S, NB, PTS), BF),
            pltpu.VMEM((K // LANES, (NB + 2 * REACH) * S, LANES), F32),
            pltpu.VMEM((K // LANES, REACH * S, LANES), F32),
            pltpu.VMEM((K // LANES, REACH * S, LANES), F32),
            pltpu.VMEM((S, NB, K), BF),
            pltpu.VMEM((NB, PTS), F32),
            pltpu.VMEM((NG, NB, GW), BF),
            pltpu.VMEM((ROWS, ROWS), BF),
            pltpu.VMEM((ROWS, ROWS), BF),
            dma((5,)),
            dma((NT,)),
            dma((NT,)),
            dma,
            dma,
            dma,
            dma,
            dma,
            dma((NT,)),
            dma,
            dma,
            dma((2,)),
            dma((2,)),
        ],
        compiler_params=pltpu.CompilerParams(
            collective_id=0, has_side_effects=True, vmem_limit_bytes=60 << 20
        ),
    )(signs[0], offsets, contrast, incident[0], adjoint[0], proj, mats, expand)

    scattered, gradient = pl.pallas_call(
        output_kernel,
        out_shape=(
            jax.ShapeDtypeStruct((S, NB, PTS), BF),
            jax.ShapeDtypeStruct((NB, GW), F32),
        ),
        in_specs=[any_spec] * 4,
        out_specs=(any_spec, any_spec),
        scratch_shapes=[
            pltpu.VMEM((S, NB, K), BF),
            pltpu.VMEM(expand.shape, BF),
            pltpu.VMEM((NG, NB, GW), BF),
            pltpu.VMEM((S, NB, PTS), BF),
            pltpu.VMEM((NB, GW), F32),
            dma((NT,)),
            dma,
            dma,
            dma((HP * ET,)),
            dma,
            dma,
        ],
        compiler_params=pltpu.CompilerParams(vmem_limit_bytes=60 << 20),
    )(local, expand, parts, ready)
    return scattered[None], gradient


def solution(mesh):
    in_specs = (
        P("tile", "group"),
        P("group", None, "tile", None),
        P("group", None, None),
        P("group", None, "tile", None),
        P(),
        P(),
        P(),
        P(),
    )
    out_specs = (P("group", None, "tile", None), P("tile", "group"))
    return jax.shard_map(
        on_device, mesh=mesh, in_specs=in_specs, out_specs=out_specs, check_vma=False
    )
```
